256 devices in a mesh: fsdp: 32 (over z_hi, y, core), tp: 8 (over z_lo, x).
Axes of the slice: x: 4, y: 4, z: 8 (z_hi: 4, z_lo: 2; z = z_hi * 2 + z_lo), core: 2. Of those that a mesh axis runs over, the one named last changes fastest.
Arguments:
- normed: bfloat16 [32768, 8192], P('fsdp'), may hold values from -6 to 6
- kv_weight: bfloat16 [8192, 2048], P('fsdp', 'tp'), may hold values from -0.0625 to 0.0625
- kv_cotangent: bfloat16 [32768, 2048], P('fsdp', 'tp'), may hold values from -0.25 to 0.25
- first_moment: float32 [8192, 2048], P('fsdp', 'tp'), may hold values from -6 to 6
- second_moment: float32 [8192, 2048], P('fsdp', 'tp'), may hold values from 0.5 to 5
- cauchy_points: int32 [20], replicated, may hold values from 0 to 19, each once
Outputs:
- keys_values: bfloat16 [32768, 2048], P('fsdp', 'tp')
- new_first: float32 [8192, 2048], P('fsdp', 'tp')
- new_second: float32 [8192, 2048], P('fsdp', 'tp')
- parity: float32 [4, 2, 4096, 256], P(None, None, 'fsdp', 'tp')
The draws below stay inside these ranges and needn't reach their ends.
Inputs may be any that keep to these rules, and one draw needn't show every extreme that they name: `cauchy_points`: each value once; the first 4 entries are the parity points, the other 16 the members' points in rank order.
All inputs are finite; a program needn't handle non-finite values.
Results may differ from the reference program's by a relative error of at most 0.001.
Values may be sent and summed in bfloat16 or wider, within the bound.
A program may use at most 192 MiB of HBM per device.

```python
import math
import jax
import jax.numpy as jnp
from jax import lax

D = 8192
GROUP = 16
PARITY = 4
KVC = 2048
TOKENS = 32768
SHARD_ROWS = 256
SHARD_COLS = 256
GROUP_FSDP = 2
N_FSDP = 32
N_TP = 8


def raised(result, rng, source, target, shards_of, factor):
    owner, partner = [(jnp.arange(result.shape[dim]) // (result.shape[dim] // shards_of)).reshape([-1 if axis == dim else 1 for axis in range(result.ndim)]) for dim in (source, target)]
    chosen = jax.random.permutation(rng, shards_of)[partner]
    strong = (owner == chosen) | (owner == (partner + shards_of // 2) % shards_of)
    return jnp.where(strong, factor * result, result)


def levels(stream_key, extent, cuts, low, top_value):
    def one(axis_at, blocks):
        steps = jax.random.uniform(jax.random.fold_in(jax.random.fold_in(stream_key, 6), axis_at), (blocks,), jnp.float32, low / len(cuts), top_value / len(cuts))
        return jnp.repeat(jnp.exp(steps), extent[axis_at] // blocks).reshape((-1,) + (1,) * (len(extent) - axis_at - 1))

    level = one(*cuts[0])
    for cut in cuts[1:]:
        level = level * one(*cut)
    return level


def gaussian(stream_key, extent, deviation, limit, cuts=(), dtype=jnp.bfloat16):
    values = jax.random.normal(stream_key, extent, jnp.float32) * deviation
    if len(cuts) > 0:
        values = levels(stream_key, extent, cuts, -0.22, 0.18) * values
    return jnp.clip(values, min=-limit, max=limit).astype(dtype)


def gaussian_with(own_key, dims, deviation, limit, split, heavy, held_as=jnp.bfloat16):
    result = deviation * jax.random.normal(own_key, dims, jnp.float32)
    if split:
        result = result * levels(own_key, dims, split, -0.22, 0.18)
    return jnp.clip(raised(result, jax.random.fold_in(own_key, 3), *heavy), -limit, limit).astype(held_as)


def setup_inputs(seed: int = 0) -> dict:
    streams_of = jax.random.split(jax.random.key(seed), 7)
    return {
        "normed": gaussian_with(streams_of[0], (TOKENS, D), 1.0, 6.0, ((0, 32),), (0, 1, 32, 2.75)),
        "kv_weight": gaussian(streams_of[1], (D, KVC), D ** -0.5, 0.0625, ((0, 32), (1, 8))),
        "kv_cotangent": gaussian(streams_of[2], (TOKENS, KVC), (8.0 / TOKENS ** 0.5), 0.25, ((0, 32), (1, 8))),
        "first_moment": gaussian(streams_of[3], (D, KVC), 1.0, 6.0, ((0, 32), (1, 8)), jnp.float32),
        "second_moment": jnp.clip(jnp.exp(math.log(5.0) - 2.3025851 * jax.random.uniform(streams_of[4], (D, KVC), jnp.float32) ** levels(streams_of[4], (D, KVC), ((0, 32), (1, 8)), -0.2, 0.2)), 0.5, 5.0),
        "cauchy_points": jax.random.permutation(streams_of[5], PARITY + GROUP).astype(jnp.int32),
    }


beta_first = 0.9
beta_second = 0.95


def reference(normed, kv_weight, kv_cotangent, first_moment, second_moment, cauchy_points):
    keys_values = jnp.dot(normed, kv_weight, preferred_element_type=jnp.float32).astype(jnp.bfloat16)
    gradient = lax.dot_general(normed, kv_cotangent, (((0,), (0,)), ((), ())), preferred_element_type=jnp.float32)
    new_first = beta_first * first_moment + (1.0 - beta_first) * gradient
    new_second = beta_second * second_moment + (1.0 - beta_second) * gradient * gradient
    points = cauchy_points.astype(jnp.float32)
    cauchy = 1.0 / (points[:PARITY, None] - points[None, PARITY:])
    blocks = N_FSDP // GROUP_FSDP
    payload = jnp.stack([new_first, new_second]).reshape(2, blocks, GROUP_FSDP, SHARD_ROWS, N_TP, SHARD_COLS)
    weights_grid = cauchy.reshape(PARITY, GROUP_FSDP, N_TP)
    parity = jnp.einsum('igt,cbgdte->icbde', weights_grid, payload, precision=lax.Precision.HIGHEST)
    parity = parity.reshape(PARITY, 2, blocks * SHARD_ROWS, SHARD_COLS)
    return keys_values, new_first, new_second, parity
```

```python
import functools

import jax
import jax.numpy as jnp
from jax import lax
from jax.experimental import pallas as pl
from jax.experimental.pallas import tpu as pltpu
from jax.sharding import PartitionSpec as P

MESH = pl.DeviceIdType.MESH
GROUP = 16
PARITY = 4
BETA_FIRST = 0.9
BETA_SECOND = 0.95
HOP = 3
FIRST = 3


def order(i):
    return i % 3 + 3 * ((3 - i) // 3)


def gray(i):
    return i + i // 2 - 2 * (i // 3)


def encode(x, out):
    n = x.shape[0]
    top = jnp.max(jnp.abs(x), axis=0, keepdims=True)
    power = jnp.ceil(jnp.log2(jnp.maximum(top, 1e-30)))
    scaled = jnp.round(x * jnp.exp2(15.0 - power))
    out[0:n, :] = jnp.clip(scaled, -32767.0, 32767.0).astype(jnp.int32).astype(jnp.int16)
    out[n : n + 16, :] = jnp.broadcast_to(power, (16, x.shape[1])).astype(jnp.int32).astype(jnp.int16)


def decode(ref):
    n = ref.shape[0] - 16
    power = ref[n : n + 16, :].astype(jnp.int32).astype(jnp.float32)[0:1, :]
    return ref[0:n, :].astype(jnp.int32).astype(jnp.float32) * jnp.exp2(power - 15.0)


def kernel(
    normed, w, cot, m1, m2, points,
    kv, nf, ns, par,
    nb, wb, cb, ct, mb, mt, sums, tmp, xs, xr, ys, yr, zs, zr, acc, ps, pr,
    n_sem, in_sem, w_sem, xs_sem, xr_sem, ys_sem, yr_sem, zs_sem, zr_sem,
    agr_sem, agy_sem, agz_sem, ags_sem, agp_sem, ps_sem, pr_sem,
):
    f, t = lax.axis_index("fsdp"), lax.axis_index("tp")
    core, chip = f % 2, f // 2
    y, z = chip % 4, chip // 4
    rank = core * 8 + t

    def at(dz, dy):
        return {"fsdp": (((z + dz) % 4) * 4 + (y + dy) % 4) * 2 + core}

    partner = {"fsdp": chip * 2 + 1 - core}
    y_to = (at(0, 1), at(0, 3))
    z_to = (at(1, 0), at(3, 0))

    def remote(src, dst, send, recv, device):
        return pltpu.make_async_remote_copy(
            src_ref=src, dst_ref=dst, send_sem=send, recv_sem=recv, device_id=device, device_id_type=MESH
        )

    def load_pair(j):
        oz, oy = order(j // 4), order(j % 4)
        column = pl.multiple_of((((z + oz) % 4) * 4 + (y + oy) % 4) * 512, 512)
        return pltpu.make_async_copy(normed.at[:, pl.ds(column, 512)], nb.at[oz * 4 + oy], n_sem.at[j])

    own_cot = pltpu.make_async_copy(cot, cb, in_sem.at[0])
    own_w = pltpu.make_async_copy(w, wb.at[0, core], in_sem.at[1])
    own_m1 = pltpu.make_async_copy(m1, mb.at[0], in_sem.at[2])
    own_m2 = pltpu.make_async_copy(m2, mb.at[1], in_sem.at[3])
    own_cot.start()
    own_w.start()
    for j in range(4):
        load_pair(j).start()
    own_m1.start()
    own_m2.start()

    barrier = pltpu.get_barrier_semaphore()
    for device in (*y_to, *z_to):
        pl.semaphore_signal(barrier, inc=1, device_id=device, device_id_type=MESH)
    for d in range(1, 16):
        peer = (rank + d) % 16
        pl.semaphore_signal(
            barrier, inc=1, device_id={"fsdp": chip * 2 + peer // 8, "tp": peer % 8}, device_id_type=MESH
        )
    own_cot.wait()
    ct[...] = cb[...].astype(jnp.float32).T.astype(jnp.bfloat16)
    acc[...] = jnp.zeros_like(acc)
    own_w.wait()
    pl.semaphore_wait(barrier, 19)

    def w_part(slot, part):
        return wb.at[slot, core] if part is None else wb.at[slot, core, pl.ds(part * 128, 128)]

    def y_copy(oz, oy, way, part):
        there = oz * 4 + (oy + (3 if way == 0 else 1)) % 4
        return remote(
            w_part(oz * 4 + oy, part),
            w_part(there, part),
            agy_sem.at[oz, way + (0 if part is None else 2)],
            agr_sem.at[there, part or 0],
            y_to[way],
        )

    def z_copy(oz, way, part):
        there = (oz + (3 if way == 0 else 1)) % 4 * 4
        return remote(
            w_part(oz * 4, part),
            w_part(there, part),
            agz_sem.at[way + (0 if part is None else 2)],
            agr_sem.at[there, part or 0],
            z_to[way],
        )

    def partner_copy(slot):
        return remote(wb.at[slot, core], wb.at[slot, core], ags_sem.at[slot], agp_sem.at[slot], partner)

    def partner_arrived(slot):
        block = wb.at[slot, 1 - core]
        remote(block, block, ags_sem.at[slot], agp_sem.at[slot], partner).wait_recv()

    def arrived(slot, part):
        block = w_part(slot, part)
        remote(block, block, agy_sem.at[0, 0], agr_sem.at[slot, part or 0], y_to[0]).wait_recv()

    def spread(oz):
        y_copy(oz, 0, 0, None).start()
        y_copy(oz, 0, 1, None).start()
        partner_copy(oz * 4).start()

    z_copy(0, 0, None).start()
    z_copy(0, 1, None).start()
    spread(0)

    def gather_z_near():
        arrived(12, None)
        z_copy(3, 0, 0).start()
        arrived(4, None)
        z_copy(1, 1, 1).start()
        spread(1)
        spread(3)

    def gather_z_far():
        arrived(8, 0)
        arrived(8, 1)
        spread(2)

    def gather_y(k):
        if k < 4:
            oz = gray(k)
            arrived(oz * 4 + 3, None)
            y_copy(oz, 3, 0, 0).start()
            arrived(oz * 4 + 1, None)
            y_copy(oz, 1, 1, 1).start()
            partner_copy(oz * 4 + 3).start()
            partner_copy(oz * 4 + 1).start()
        if k > 0:
            oz = gray(k - 1)
            arrived(oz * 4 + 2, 0)
            arrived(oz * 4 + 2, 1)
            partner_copy(oz * 4 + 2).start()

    def x_copy(slot):
        return remote(xs.at[slot], xr.at[slot], xs_sem.at[slot], xr_sem.at[slot], partner)

    def yh_copy(way, oz, s):
        return remote(
            ys.at[way, oz, s], yr.at[way, oz, s], ys_sem.at[way, oz, s], yr_sem.at[way, oz, s], y_to[way]
        )

    def zh_copy(way, s):
        return remote(zs.at[way, s], zr.at[way, s], zs_sem.at[way, s], zr_sem.at[way, s], z_to[way])

    def half(way):
        return slice(way * 128, way * 128 + 128)

    def gradient(j):
        slot = order(j // 4) * 4 + order(j % 4)

        @pl.when(j + 4 < 16)
        def _():
            load_pair(j + 4).start()

        load_pair(j).wait()
        pair = jnp.dot(ct[...], nb[slot], preferred_element_type=jnp.float32)
        tmp[0] = pair[:, 0:256]
        tmp[1] = pair[:, 256:512]
        encode(tmp[1 - core], xs.at[slot])
        x_copy(slot).start()
        sums[slot] = tmp[core]

    def add_partner(j):
        slot = order(j // 4) * 4 + order(j % 4)
        x_copy(slot).wait_recv()
        sums[slot] += decode(xr.at[slot])

    def y_hop(g, s):
        oz = order(g)
        for way in range(2):
            if s > 0:
                yh_copy(way, oz, s - 1).wait_recv()
            slot = oz * 4 + (3 - s if way == 0 else (s + 1) % 4)
            x = sums[slot, :, half(way)]
            if s > 0:
                x = x + decode(yr.at[way, oz, s - 1])
            if s < 3:
                encode(x, ys.at[way, oz, s])
                yh_copy(way, oz, s).start()
            else:
                sums[slot, :, half(way)] = x

    def z_hop(way, s):
        oz = 3 - s if way == 0 else s + 1
        x = sums[oz * 4, :, half(way)]
        if s > 0:
            zh_copy(way, s - 1).wait_recv()
            x = x + decode(zr.at[way, s - 1])
        encode(x, zs.at[way, s])
        zh_copy(way, s).start()

    def transpose_moments():
        own_m1.wait()
        own_m2.wait()
        mt[0] = mb[0].T
        mt[1] = mb[1].T

    def p_copy(d):
        peer = (rank + d) % 16
        return remote(
            ps.at[peer // 8, peer % 8],
            pr.at[rank],
            ps_sem.at[d],
            pr_sem.at[rank],
            {"fsdp": chip * 2 + peer // 8, "tp": peer % 8},
        )

    def update():
        for way in range(2):
            zh_copy(way, 2).wait_recv()
            g = sums[0, :, half(way)] + decode(zr.at[way, 2])
            first = BETA_FIRST * mt[0, :, half(way)] + (1.0 - BETA_FIRST) * g
            second = BETA_SECOND * mt[1, :, half(way)] + (1.0 - BETA_SECOND) * g * g
            mt[0, :, half(way)] = first
            mt[1, :, half(way)] = second
            ps[way, :, 0] = first.reshape(8, 32, 128)
            ps[way, :, 1] = second.reshape(8, 32, 128)
        lax.fori_loop(1, 16, lambda d, c: (p_copy(d).start(), c)[1], 0)
        pr[rank] = ps[core, t]
        nf[...] = mt[0].T
        ns[...] = mt[1].T

    def project(q):
        slot = gray(q // 4) * 4 + gray(q % 4)
        partner_arrived(slot)
        acc[...] += jnp.dot(nb[slot], wb[slot].reshape(512, 256), preferred_element_type=jnp.float32)

    def events(j, low, high):
        def when(step, what):
            if low <= step < high:

                @pl.when(j == step)
                def _():
                    what()

        for s in range(4):
            start = FIRST + HOP * s
            if start < high and start + 12 >= low:

                @pl.when((j >= start) & (j <= start + 12) & ((j + 16 - start) % 4 == 0))
                def _():
                    y_hop((j - start) // 4, s)

        done = FIRST + HOP * 3
        when(4, lambda: gather_y(0))
        when(6, gather_z_near)
        when(9, gather_z_far)
        when(10, lambda: gather_y(1))
        when(13, lambda: gather_y(2))
        when(16, lambda: gather_y(3))
        when(20, lambda: gather_y(4))
        when(8, transpose_moments)
        when(done, lambda: z_hop(0, 0))
        when(done + 4, lambda: z_hop(1, 0))
        when(done + 8, lambda: (z_hop(0, 1), z_hop(1, 1)))
        when(done + 12, lambda: (z_hop(0, 2), z_hop(1, 2)))
        when(done + 15, update)

    def first_loop(j, carry):
        gradient(j)

        @pl.when(j >= 2)
        def _():
            add_partner(j - 2)

        events(j, 0, 16)
        return carry

    lax.fori_loop(0, 16, first_loop, 0)
    add_partner(14)
    add_partner(15)

    def second_loop(j, carry):
        project(j - 16)
        events(j, 16, 32)
        return carry

    lax.fori_loop(16, 32, second_loop, 0)
    kv[...] = acc[...].astype(jnp.bfloat16)

    par[...] = jnp.zeros_like(par)

    def member(d, carry):
        r = (rank + 16 - d) % 16

        @pl.when(d > 0)
        def _():
            remote(ps.at[core, t], pr.at[r], ps_sem.at[d], pr_sem.at[r], partner).wait_recv()

        block = pr[r]
        for i in range(PARITY):
            gap = jnp.full((32, 128), points[i] - points[PARITY + r], jnp.int32).astype(jnp.float32)
            par[i] += (1.0 / gap) * block
        return carry

    lax.fori_loop(0, 16, member, 0)

    def sent_slot(slot, carry):
        x_copy(slot).wait_send()
        partner_copy(slot).wait_send()
        return carry

    lax.fori_loop(0, 16, sent_slot, 0)
    for way in range(2):
        for oz in range(4):
            y_copy(oz, 0, way, None).wait_send()
            y_copy(oz, 3 if way == 0 else 1, way, way).wait_send()
            for s in range(3):
                yh_copy(way, oz, s).wait_send()
        z_copy(0, way, None).wait_send()
        z_copy(3 if way == 0 else 1, way, way).wait_send()
        for s in range(3):
            zh_copy(way, s).wait_send()
    lax.fori_loop(1, 16, lambda d, c: (p_copy(d).wait_send(), c)[1], 0)


def local(normed, kv_weight, kv_cotangent, first_moment, second_moment, cauchy_points):
    anywhere = pl.BlockSpec(memory_space=pl.ANY)
    vmem = pl.BlockSpec(memory_space=pltpu.VMEM)
    dma = pltpu.SemaphoreType.DMA
    kv, nf, ns, par = pl.pallas_call(
        kernel,
        out_shape=(
            jax.ShapeDtypeStruct((1024, 256), jnp.bfloat16),
            jax.ShapeDtypeStruct((256, 256), jnp.float32),
            jax.ShapeDtypeStruct((256, 256), jnp.float32),
            jax.ShapeDtypeStruct((PARITY, 2, 32, 128), jnp.float32),
        ),
        in_specs=[anywhere] * 5 + [pl.BlockSpec(memory_space=pltpu.SMEM)],
        out_specs=(vmem,) * 4,
        scratch_shapes=[
            pltpu.VMEM((16, 1024, 512), jnp.bfloat16),
            pltpu.VMEM((16, 2, 256, 256), jnp.bfloat16),
            pltpu.VMEM((1024, 256), jnp.bfloat16),
            pltpu.VMEM((256, 1024), jnp.bfloat16),
            pltpu.VMEM((2, 256, 256), jnp.float32),
            pltpu.VMEM((2, 256, 256), jnp.float32),
            pltpu.VMEM((16, 256, 256), jnp.float32),
            pltpu.VMEM((2, 256, 256), jnp.float32),
            pltpu.VMEM((16, 272, 256), jnp.int16),
            pltpu.VMEM((16, 272, 256), jnp.int16),
            pltpu.VMEM((2, 4, 3, 272, 128), jnp.int16),
            pltpu.VMEM((2, 4, 3, 272, 128), jnp.int16),
            pltpu.VMEM((2, 3, 272, 128), jnp.int16),
            pltpu.VMEM((2, 3, 272, 128), jnp.int16),
            pltpu.VMEM((1024, 256), jnp.float32),
            pltpu.VMEM((2, 8, 2, 32, 128), jnp.float32),
            pltpu.VMEM((16, 2, 32, 128), jnp.float32),
            dma((16,)),
            dma((4,)),
            dma((1,)),
            dma((16,)),
            dma((16,)),
            dma((2, 4, 3)),
            dma((2, 4, 3)),
            dma((2, 3)),
            dma((2, 3)),
            dma((16, 2)),
            dma((4, 4)),
            dma((4,)),
            dma((16,)),
            dma((16,)),
            dma((16,)),
            dma((16,)),
        ],
        compiler_params=pltpu.CompilerParams(
            collective_id=0, has_side_effects=True, vmem_limit_bytes=60 * 1024 * 1024
        ),
    )(normed, kv_weight, kv_cotangent, first_moment, second_moment, cauchy_points)
    return kv, nf, ns, par.transpose(0, 1, 3, 2)


def solution(mesh):
    return jax.shard_map(
        local,
        mesh=mesh,
        in_specs=(
            P("fsdp", None),
            P("fsdp", "tp"),
            P("fsdp", "tp"),
            P("fsdp", "tp"),
            P("fsdp", "tp"),
            P(),
        ),
        out_specs=(P("fsdp", "tp"), P("fsdp", "tp"), P("fsdp", "tp"), P(None, None, "fsdp", "tp")),
        check_vma=False,
    )
```

```python
import jax
import jax.numpy as jnp
from jax import lax
from jax.experimental import pallas as pl
from jax.experimental.pallas import tpu as pltpu
from jax.sharding import PartitionSpec as P

MESH = pl.DeviceIdType.MESH
GROUP = 16
PARITY = 4
BETA_FIRST = 0.9
BETA_SECOND = 0.95
FULL = 32766.0 / 32768.0


ORDER = (2, 3, 1, 0)


def power_of(top):
    return jnp.ceil(jnp.log2(jnp.maximum(top, 1e-30)))


def to_code(x, power):
    return to_int16(jnp.round(x * (jnp.exp2(15.0 - power) * FULL)))


def step_of(power):
    return jnp.exp2(power - 15.0) * (1.0 / FULL)


def to_int16(x):
    return x.astype(jnp.int32).astype(jnp.int16)


def to_float(x):
    return x.astype(jnp.int32).astype(jnp.float32)


def encode(x, out):
    n = x.shape[0]
    power = power_of(jnp.max(jnp.abs(x), axis=0, keepdims=True))
    out[0:n, :] = to_code(x, power)
    out[n : n + 16, :] = to_int16(jnp.broadcast_to(power, (16, x.shape[1])))


def decode(ref):
    n = ref.shape[0] - 16
    power = to_float(ref[n : n + 16, :])[0:1, :]
    return to_float(ref[0:n, :]) * step_of(power)


def encode_blocks(x, kind, powers, out):
    blocks = x.reshape(8, 32, 128)
    power = power_of(jnp.max(jnp.abs(blocks), axis=1, keepdims=True))
    out[:, kind * 32 : kind * 32 + 32, :] = to_code(blocks, power)
    powers.append(power)


def encode_powers(powers, out):
    low = lax.broadcasted_iota(jnp.int32, (8, 16, 128), 1) < 8
    out[:, 64:80, :] = to_int16(jnp.where(low, powers[0], powers[1]))


def decode_block(ref):
    powers = to_float(ref[64:80, :])
    return [
        to_float(ref[kind * 32 : kind * 32 + 32, :]) * step_of(powers[kind * 8 : kind * 8 + 1, :])
        for kind in range(2)
    ]


def kernel(
    normed, w, cot, m1, m2, cauchy_points,
    kv, nf, ns, par,
    nb, wb, cb, ct, mb, mt, sums, tmp, xs, xr, ys, yr, zs, zr, acc, ps, pr, points,
    n_sem, in_sem, xs_sem, xr_sem, ys_sem, yr_sem, zs_sem, zr_sem,
    agr_sem, agy_sem, agz_sem, ags_sem, agp_sem, ps_sem, pr_sem,
):
    f, t = lax.axis_index("fsdp"), lax.axis_index("tp")
    core, chip = f & 1, f >> 1
    y, z = chip & 3, chip >> 2
    rank = core * 8 + t

    def at(dz, dy):
        return {"fsdp": ((((z + dz) & 3) << 2) + ((y + dy) & 3)) * 2 + core}

    def member_at(peer):
        return {"fsdp": chip * 2 + (peer >> 3), "tp": peer & 7}

    partner = {"fsdp": chip * 2 + 1 - core}
    y_to = (at(0, 1), at(0, 3))
    z_to = (at(1, 0), at(3, 0))

    def remote(src, dst, send, recv, device):
        return pltpu.make_async_remote_copy(
            src_ref=src, dst_ref=dst, send_sem=send, recv_sem=recv, device_id=device, device_id_type=MESH
        )

    def load_pair(slot, column):
        return pltpu.make_async_copy(normed.at[:, pl.ds(column, 512)], nb.at[slot], n_sem.at[slot])

    own_cot = pltpu.make_async_copy(cot, cb, in_sem.at[0])
    own_w = pltpu.make_async_copy(w, wb.at[15, core], in_sem.at[1])
    own_m1 = pltpu.make_async_copy(m1, mb.at[0], in_sem.at[2])
    own_m2 = pltpu.make_async_copy(m2, mb.at[1], in_sem.at[3])
    own_points = pltpu.make_async_copy(cauchy_points, points, in_sem.at[4])

    def w_part(slot, part):
        return wb.at[slot, core] if part is None else wb.at[slot, core, pl.ds(part * 128, 128)]

    def w_copy(slot, there, way, part, send, device):
        return remote(w_part(slot, part), w_part(there, part), send.at[slot, way], agr_sem.at[there, part or 0], device)

    def y_copy(base, place, way):
        to = {(3, 0): 1, (3, 1): 2, (1, 0): 0, (2, 1): 0}[place, way]
        return w_copy(base + place, base + to, way, None if place == 3 else way, agy_sem, y_to[way])

    def z_copy(slot, way):
        there = {(15, 0): 7, (15, 1): 11, (7, 0): 3, (11, 1): 3}[slot, way]
        return w_copy(slot, there, way, None if slot == 15 else way, agz_sem, z_to[way])

    def partner_copy(slot):
        return remote(wb.at[slot, core], wb.at[slot, core], ags_sem.at[slot], agp_sem.at[slot], partner)

    def partner_arrived(slot):
        block = wb.at[slot, 1 - core]
        remote(block, block, ags_sem.at[slot], agp_sem.at[slot], partner).wait_recv()

    def arrived(slot, part):
        block = w_part(slot, part)
        remote(block, block, agy_sem.at[0, 0], agr_sem.at[slot, part or 0], y_to[0]).wait_recv()

    def spread(base):
        y_copy(base, 3, 0).start()
        y_copy(base, 3, 1).start()

    def gather_start():
        own_w.wait()
        z_copy(15, 0).start()
        z_copy(15, 1).start()
        spread(12)
        partner_copy(15).start()

    def gather_z_near():
        arrived(7, None)
        z_copy(7, 0).start()
        arrived(11, None)
        z_copy(11, 1).start()
        partner_copy(7).start()
        partner_copy(11).start()

    def gather_z_far():
        arrived(3, 0)
        arrived(3, 1)
        partner_copy(3).start()

    def gather_y_near(base):
        arrived(base + 1, None)
        y_copy(base, 1, 0).start()
        arrived(base + 2, None)
        y_copy(base, 2, 1).start()
        partner_copy(base + 1).start()
        partner_copy(base + 2).start()

    def gather_y_far(base):
        arrived(base, 0)
        arrived(base, 1)
        partner_copy(base).start()

    def x_copy(slot):
        return remote(xs.at[slot], xr.at[slot], xs_sem.at[slot], xr_sem.at[slot], partner)

    def ysum_copy(way, g, s):
        return remote(ys.at[way, g, s], yr.at[way, g, s], ys_sem.at[way, g, s], yr_sem.at[way, g, s], y_to[way])

    def zsum_copy(way, s):
        return remote(zs.at[way, s], zr.at[way, s], zs_sem.at[way, s], zr_sem.at[way, s], z_to[way])

    def half(way):
        return slice(way * 128, way * 128 + 128)

    def gradient(j):
        load_pair(j, 0).wait()
        pair = jnp.dot(ct[...], nb[j], preferred_element_type=jnp.float32)
        tmp[0] = pair[:, 0:256]
        tmp[1] = pair[:, 256:512]
        encode(tmp[1 - core], xs.at[j])

        @pl.when(j == 0)
        def _():
            pl.semaphore_wait(barrier, 19)
            gather_start()

        x_copy(j).start()
        sums[j] = tmp[core]

    def add_partner(j):
        x_copy(j).wait_recv()
        sums[j] += decode(xr.at[j])

    def y_sum(g, s):
        base = g * 4
        for way in range(2):
            near = base + 2 - way
            if s == 0:
                encode(sums[base, :, half(way)], ys.at[way, g, 0])
            elif s == 1:
                encode(sums[near, :, half(1 - way)], ys.at[way, g, 1])
            elif s == 2:
                ysum_copy(way, g, 0).wait_recv()
                encode(sums[near, :, half(way)] + decode(yr.at[way, g, 0]), ys.at[way, g, 2])
            else:
                ysum_copy(1 - way, g, 1).wait_recv()
                ysum_copy(way, g, 2).wait_recv()
                sums[base + 3, :, half(way)] += decode(yr.at[1 - way, g, 1]) + decode(yr.at[way, g, 2])
            if s < 3:
                ysum_copy(way, g, s).start()

    def z_antipode():
        for way in range(2):
            encode(sums[3, :, half(way)], zs.at[way, 0])
            zsum_copy(way, 0).start()

    def z_free(way):
        encode(sums[11 if way == 0 else 7, :, half(1 - way)], zs.at[way, 1])
        zsum_copy(way, 1).start()

    def z_joined(way):
        zsum_copy(way, 0).wait_recv()
        encode(sums[11 if way == 0 else 7, :, half(way)] + decode(zr.at[way, 0]), zs.at[way, 2])
        zsum_copy(way, 2).start()

    def transpose_moments():
        own_m1.wait()
        own_m2.wait()
        own_points.wait()
        mt[0] = mb[0].T
        mt[1] = mb[1].T

    def p_copy(d):
        peer = (rank + d) & 15
        return remote(ps.at[peer >> 3, peer & 7], pr.at[rank], ps_sem.at[d], pr_sem.at[rank], member_at(peer))

    def update():
        for way in range(2):
            zsum_copy(1 - way, 1).wait_recv()
            zsum_copy(way, 2).wait_recv()
            g = sums[15, :, half(way)] + (decode(zr.at[1 - way, 1]) + decode(zr.at[way, 2]))
            first = BETA_FIRST * mt[0, :, half(way)] + (1.0 - BETA_FIRST) * g
            second = BETA_SECOND * mt[1, :, half(way)] + (1.0 - BETA_SECOND) * g * g
            mt[0, :, half(way)] = first
            mt[1, :, half(way)] = second
            powers = []
            encode_blocks(first, 0, powers, ps.at[way])
            encode_blocks(second, 1, powers, ps.at[way])
            encode_powers(powers, ps.at[way])
        lax.fori_loop(1, 16, lambda d, c: (p_copy(d).start(), c)[1], 0)
        pr[rank] = ps[core, t]
        nf[...] = mt[0].T
        ns[...] = mt[1].T

    def project(slot):
        partner_arrived(slot)
        acc[...] += jnp.dot(nb[slot], wb[slot].reshape(512, 256), preferred_element_type=jnp.float32)

    actions = {
        "near_0": lambda: gather_y_near(12),
        "far_0": lambda: gather_y_far(12),
        "z_near": gather_z_near,
        "z_far": gather_z_far,
        "moments": transpose_moments,
        "z_antipode": z_antipode,
        "z_free_1": lambda: z_free(1),
        "z_joined_1": lambda: z_joined(1),
        "z_free_0": lambda: z_free(0),
        "z_joined_0": lambda: z_joined(0),
        "spread_1": lambda: spread(8),
        "spread_2": lambda: spread(4),
        "spread_3": lambda: spread(0),
    }

    def events(j, low, high):
        for s in range(4):
            start = Y_STEPS[s]
            if start < high and start + 12 >= low:

                @pl.when((j >= start) & (j <= start + 12) & (((j - start) & 3) == 0))
                def _():
                    y_sum((j - start) >> 2, s)

        for step, names in STEPS.items():
            if low <= step < high:

                @pl.when(j == step)
                def _():
                    for name in names:
                        actions[name]()

    own_cot.start()
    rows = [((z + oz) & 3) << 11 for oz in ORDER]
    places = [((y + oy) & 3) << 9 for oy in ORDER]
    loads = [load_pair(4 * g + i, pl.multiple_of(rows[g] + places[i], 512)) for g in range(4) for i in range(4)]
    loads[0].start()
    own_w.start()
    for load in loads[1:]:
        load.start()
    own_m1.start()
    own_m2.start()
    own_points.start()

    barrier = pltpu.get_barrier_semaphore()
    for device in (*y_to, *z_to):
        pl.semaphore_signal(barrier, inc=1, device_id=device, device_id_type=MESH)
    for d in range(1, 16):
        pl.semaphore_signal(barrier, inc=1, device_id=member_at((rank + d) & 15), device_id_type=MESH)
    own_cot.wait()
    ct[...] = cb[...].astype(jnp.float32).T.astype(jnp.bfloat16)

    def first_loop(j, carry):
        gradient(j)

        @pl.when(j >= 2)
        def _():
            add_partner(j - 2)

        events(j, 0, 16)
        return carry

    lax.fori_loop(0, 16, first_loop, 0)
    acc[...] = jnp.zeros_like(acc)
    par[...] = jnp.zeros_like(par)

    def second_loop(j, carry):
        @pl.when(j < 18)
        def _():
            add_partner(j - 2)

        events(j, 16, LAST)

        @pl.when((j >= PROJECT) & (j < PROJECT + 4))
        def _():
            project(15 + PROJECT - j)

        return carry

    lax.fori_loop(16, LAST, second_loop, 0)
    update()

    def near_loop(k, carry):
        base = 12 - 4 * k
        gather_y_near(base)

        def three(i, inner):
            project(base + 3 - i)
            return inner

        return lax.fori_loop(0, 3, three, carry)

    def far_loop(k, carry):
        gather_y_far(12 - 4 * k)
        project(12 - 4 * k)
        return carry

    lax.fori_loop(1, 4, near_loop, 0)
    lax.fori_loop(1, 4, far_loop, 0)
    kv[...] = acc[...].astype(jnp.bfloat16)

    def member(d, carry):
        r = (rank + 16 - d) & 15

        @pl.when(d > 0)
        def _():
            remote(ps.at[core, t], pr.at[r], ps_sem.at[d], pr_sem.at[r], partner).wait_recv()

        blocks = decode_block(pr.at[r])
        for i in range(PARITY):
            gap = jnp.full((32, 128), points[i] - points[PARITY + r], jnp.int32).astype(jnp.float32)
            weight = 1.0 / gap
            for kind in range(2):
                par[i, kind] += weight * blocks[kind]
        return carry

    lax.fori_loop(0, 16, member, 0)

    def sent_slot(slot, carry):
        x_copy(slot).wait_send()
        partner_copy(slot).wait_send()
        return carry

    def sent_group(g, carry):
        for way in range(2):
            y_copy(4 * g, 3, way).wait_send()
            y_copy(4 * g, 1 + way, way).wait_send()
            for s in range(3):
                ysum_copy(way, g, s).wait_send()
        return carry

    lax.fori_loop(0, 16, sent_slot, 0)
    lax.fori_loop(0, 4, sent_group, 0)
    for way in range(2):
        z_copy(15, way).wait_send()
        z_copy(7 if way == 0 else 11, way).wait_send()
        for s in range(3):
            zsum_copy(way, s).wait_send()
    lax.fori_loop(1, 16, lambda d, c: (p_copy(d).wait_send(), c)[1], 0)


Y_STEPS = (2, 4, 6, 10)
STEPS = {
    5: ("near_0",),
    8: ("z_near", "moments"),
    9: ("far_0",),
    10: ("z_antipode",),
    13: ("z_far",),
    14: ("z_free_1",),
    16: ("z_joined_1",),
    18: ("z_free_0", "z_joined_0", "spread_1", "spread_2", "spread_3"),
}
PROJECT = 17
LAST = 23


def hand_out(*refs):
    half = len(refs) // 2
    for source, target in zip(refs[:half], refs[half:]):
        target[...] = source[...]


def local(normed, kv_weight, kv_cotangent, first_moment, second_moment, cauchy_points):
    hbm = pl.BlockSpec(memory_space=pltpu.HBM)
    vmem = pl.BlockSpec(memory_space=pltpu.VMEM)
    dma = pltpu.SemaphoreType.DMA
    shapes = (
        jax.ShapeDtypeStruct((1024, 256), jnp.bfloat16),
        jax.ShapeDtypeStruct((256, 256), jnp.float32),
        jax.ShapeDtypeStruct((256, 256), jnp.float32),
        jax.ShapeDtypeStruct((PARITY, 2, 32, 128), jnp.float32),
    )
    results = pl.pallas_call(
        kernel,
        out_shape=shapes,
        in_specs=[hbm] * 6,
        out_specs=(vmem,) * 4,
        scratch_shapes=[
            pltpu.VMEM((16, 1024, 512), jnp.bfloat16),
            pltpu.VMEM((16, 2, 256, 256), jnp.bfloat16),
            pltpu.VMEM((1024, 256), jnp.bfloat16),
            pltpu.VMEM((256, 1024), jnp.bfloat16),
            pltpu.VMEM((2, 256, 256), jnp.float32),
            pltpu.VMEM((2, 256, 256), jnp.float32),
            pltpu.VMEM((16, 256, 256), jnp.float32),
            pltpu.VMEM((2, 256, 256), jnp.float32),
            pltpu.VMEM((16, 272, 256), jnp.int16),
            pltpu.VMEM((16, 272, 256), jnp.int16),
            pltpu.VMEM((2, 4, 3, 272, 128), jnp.int16),
            pltpu.VMEM((2, 4, 3, 272, 128), jnp.int16),
            pltpu.VMEM((2, 3, 272, 128), jnp.int16),
            pltpu.VMEM((2, 3, 272, 128), jnp.int16),
            pltpu.VMEM((1024, 256), jnp.float32),
            pltpu.VMEM((2, 8, 80, 128), jnp.int16),
            pltpu.VMEM((16, 80, 128), jnp.int16),
            pltpu.SMEM((20,), jnp.int32),
            dma((16,)),
            dma((5,)),
            dma((16,)),
            dma((16,)),
            dma((2, 4, 3)),
            dma((2, 4, 3)),
            dma((2, 3)),
            dma((2, 3)),
            dma((16, 2)),
            dma((16, 2)),
            dma((16, 2)),
            dma((16,)),
            dma((16,)),
            dma((16,)),
            dma((16,)),
        ],
        compiler_params=pltpu.CompilerParams(
            collective_id=0, has_side_effects=True, vmem_limit_bytes=46 * 1024 * 1024
        ),
    )(*[pltpu.with_memory_space_constraint(v, pltpu.HBM) for v in (normed, kv_weight, kv_cotangent, first_moment, second_moment, cauchy_points)])
    kv, nf, ns, par = pl.pallas_call(
        hand_out,
        out_shape=shapes,
        in_specs=[vmem] * 4,
        out_specs=(vmem,) * 4,
        compiler_params=pltpu.CompilerParams(vmem_limit_bytes=8 * 1024 * 1024),
    )(*results)
    return kv, nf, ns, par.transpose(0, 1, 3, 2)


def solution(mesh):
    return jax.shard_map(
        local,
        mesh=mesh,
        in_specs=(
            P("fsdp", None),
            P("fsdp", "tp"),
            P("fsdp", "tp"),
            P("fsdp", "tp"),
            P("fsdp", "tp"),
            P(),
        ),
        out_specs=(P("fsdp", "tp"), P("fsdp", "tp"), P("fsdp", "tp"), P(None, None, "fsdp", "tp")),
        check_vma=False,
    )
```

```python
import jax
import jax.numpy as jnp
from jax import lax
from jax.experimental import pallas as pl
from jax.experimental.pallas import tpu as pltpu
from jax.sharding import PartitionSpec as P

MESH = pl.DeviceIdType.MESH
GROUP = 16
PARITY = 4
BETA_FIRST = 0.9
BETA_SECOND = 0.95
FULL = 32766.0 / 32768.0


SEQUENCE = (
    *((2, 2), (2, 3), (2, 1), (2, 0)),
    *((1, 2), (3, 2), (1, 3), (3, 3), (1, 1), (3, 1), (1, 0), (3, 0)),
    *((0, 2), (0, 3), (0, 1), (0, 0)),
)
SLOT = {chip: slot for slot, chip in enumerate(SEQUENCE)}
HALVES = ((2, 2), (1, 3), (3, 1), (0, 0))


def power_of(top):
    return jnp.ceil(jnp.log2(jnp.maximum(top, 1e-30)))


def to_code(x, power):
    return to_int16(jnp.round(x * (jnp.exp2(15.0 - power) * FULL)))


def step_of(power):
    return jnp.exp2(power - 15.0) * (1.0 / FULL)


def to_int16(x):
    return x.astype(jnp.int32).astype(jnp.int16)


def to_float(x):
    return x.astype(jnp.int32).astype(jnp.float32)


def encode(x, out):
    n = x.shape[0]
    power = power_of(jnp.max(jnp.abs(x), axis=0, keepdims=True))
    out[0:n, :] = to_code(x, power)
    out[n : n + 16, :] = to_int16(jnp.broadcast_to(power, (16, x.shape[1])))


def decode(ref):
    n = ref.shape[0] - 16
    power = to_float(ref[n : n + 16, :])[0:1, :]
    return to_float(ref[0:n, :]) * step_of(power)


def encode_blocks(x, kind, powers, out):
    blocks = x.reshape(8, 32, 128)
    power = power_of(jnp.max(jnp.abs(blocks), axis=1, keepdims=True))
    out[:, kind * 32 : kind * 32 + 32, :] = to_code(blocks, power)
    powers.append(power)


def encode_powers(powers, out):
    low = lax.broadcasted_iota(jnp.int32, (8, 16, 128), 1) < 8
    out[:, 64:80, :] = to_int16(jnp.where(low, powers[0], powers[1]))


def decode_block(ref):
    powers = to_float(ref[64:80, :])
    return [
        to_float(ref[kind * 32 : kind * 32 + 32, :]) * step_of(powers[kind * 8 : kind * 8 + 1, :])
        for kind in range(2)
    ]


def kernel(
    normed, w, cot, m1, m2, cauchy_points,
    kv, nf, ns, par,
    nb, wb, cb, ct, mb, mt, sums, xs, xr, ys, yr, zs, zr, acc, ps, pr, points,
    n_sem, in_sem, xs_sem, xr_sem, ys_sem, yr_sem, zs_sem, zr_sem,
    agr_sem, agy_sem, agz_sem, ags_sem, agp_sem, ps_sem, pr_sem,
):
    f, t = lax.axis_index("fsdp"), lax.axis_index("tp")
    core, chip = f & 1, f >> 1
    y, z = chip & 3, chip >> 2
    rank = core * 8 + t

    def at(dz, dy):
        return {"fsdp": ((((z + dz) & 3) << 2) + ((y + dy) & 3)) * 2 + core}

    def member_at(peer):
        return {"fsdp": chip * 2 + (peer >> 3), "tp": peer & 7}

    partner = {"fsdp": chip * 2 + 1 - core}
    y_to = (at(0, 1), at(0, 3))
    z_to = (at(1, 0), at(3, 0))

    def remote(src, dst, send, recv, device):
        return pltpu.make_async_remote_copy(
            src_ref=src, dst_ref=dst, send_sem=send, recv_sem=recv, device_id=device, device_id_type=MESH
        )

    def load_pair(slot, column):
        return pltpu.make_async_copy(normed.at[:, pl.ds(column, 512)], nb.at[slot], n_sem.at[slot])

    own_cot = pltpu.make_async_copy(cot, cb, in_sem.at[0])
    own_w = pltpu.make_async_copy(w, wb.at[SLOT[0, 0], core], in_sem.at[1])
    own_m1 = pltpu.make_async_copy(m1, mb.at[0], in_sem.at[2])
    own_m2 = pltpu.make_async_copy(m2, mb.at[1], in_sem.at[3])
    own_points = pltpu.make_async_copy(cauchy_points, points, in_sem.at[4])

    def w_part(slot, part):
        return wb.at[slot, core] if part is None else wb.at[slot, core, pl.ds(part * 128, 128)]

    def w_copy(slot, there, way, part, send, device):
        return remote(w_part(slot, part), w_part(there, part), send.at[slot, way], agr_sem.at[there, part or 0], device)

    onward = {(0, 0): 3, (0, 1): 1, (3, 0): 2, (1, 1): 2}

    def y_copy(oz, oy, way):
        there = SLOT[oz, onward[oy, way]]
        return w_copy(SLOT[oz, oy], there, way, way if oy else None, agy_sem, y_to[way])

    def z_copy(oz, way):
        there = SLOT[onward[oz, way], 0]
        return w_copy(SLOT[oz, 0], there, way, way if oz else None, agz_sem, z_to[way])

    def partner_copy(slot):
        return remote(wb.at[slot, core], wb.at[slot, core], ags_sem.at[slot], agp_sem.at[slot], partner)

    def partner_arrived(slot):
        block = wb.at[slot, 1 - core]
        remote(block, block, ags_sem.at[slot], agp_sem.at[slot], partner).wait_recv()

    def arrived(slot, part):
        block = w_part(slot, part)
        remote(block, block, agy_sem.at[0, 0], agr_sem.at[slot, part or 0], y_to[0]).wait_recv()

    def spread(oz):
        y_copy(oz, 0, 0).start()
        y_copy(oz, 0, 1).start()

    def gather_start():
        own_w.wait()
        z_copy(0, 0).start()
        z_copy(0, 1).start()
        spread(0)
        partner_copy(SLOT[0, 0]).start()

    def z_near():
        arrived(SLOT[3, 0], None)
        z_copy(3, 0).start()
        arrived(SLOT[1, 0], None)
        z_copy(1, 1).start()
        partner_copy(SLOT[3, 0]).start()
        partner_copy(SLOT[1, 0]).start()

    def z_far():
        arrived(SLOT[2, 0], 0)
        arrived(SLOT[2, 0], 1)
        partner_copy(SLOT[2, 0]).start()

    def y_near(oz):
        arrived(SLOT[oz, 3], None)
        y_copy(oz, 3, 0).start()
        arrived(SLOT[oz, 1], None)
        y_copy(oz, 1, 1).start()
        partner_copy(SLOT[oz, 3]).start()
        partner_copy(SLOT[oz, 1]).start()

    def y_far(oz):
        arrived(SLOT[oz, 2], 0)
        arrived(SLOT[oz, 2], 1)
        partner_copy(SLOT[oz, 2]).start()

    def x_copy(slot):
        return remote(xs.at[slot], xr.at[slot], xs_sem.at[slot], xr_sem.at[slot], partner)

    def ysum_copy(way, g, s):
        return remote(ys.at[way, g, s], yr.at[way, g, s], ys_sem.at[way, g, s], yr_sem.at[way, g, s], y_to[way])

    def zsum_copy(way, s):
        return remote(zs.at[way, s], zr.at[way, s], zs_sem.at[way, s], zr_sem.at[way, s], z_to[way])

    def half(way):
        return slice(way * 128, way * 128 + 128)

    def gradient(j):
        load_pair(j, 0).wait()
        pair = jnp.dot(ct[...], nb[j], preferred_element_type=jnp.float32)
        sums[j, 0] = pair[:, 0:256]
        sums[j, 1] = pair[:, 256:512]
        encode(sums[j, 1 - core], xs.at[j])

        @pl.when(j == 0)
        def _():
            pl.semaphore_wait(barrier, 19)
            gather_start()

        x_copy(j).start()

    def add_partner(j):
        x_copy(j).wait_recv()
        sums[j, core] += decode(xr.at[j])

    def y_sum(g, s):
        for way in range(2):
            part = 1 - way if s == 1 else way
            oy = (2, 1 if way == 0 else 3, 1 if way == 0 else 3, 0)[s]
            slot = SLOT[HALVES[g][part], oy]
            x = sums[slot, core, :, half(part)]
            if s == 2:
                ysum_copy(way, g, 0).wait_recv()
                x = x + decode(yr.at[way, g, 0])
            if s == 3:
                ysum_copy(1 - way, g, 1).wait_recv()
                ysum_copy(way, g, 2).wait_recv()
                sums[slot, core, :, half(part)] = x + (decode(yr.at[1 - way, g, 1]) + decode(yr.at[way, g, 2]))
            else:
                encode(x, ys.at[way, g, s])
                ysum_copy(way, g, s).start()

    def z_sum(s):
        for way in range(2):
            part = 1 - way if s == 1 else way
            oz = 2 if s == 0 else 1 if way == 0 else 3
            x = sums[SLOT[oz, 0], core, :, half(part)]
            if s == 2:
                zsum_copy(way, 0).wait_recv()
                x = x + decode(zr.at[way, 0])
            encode(x, zs.at[way, s])
            zsum_copy(way, s).start()

    def transpose_moments():
        own_m1.wait()
        own_m2.wait()
        own_points.wait()
        mt[0] = mb[0].T
        mt[1] = mb[1].T

    def p_copy(d):
        peer = (rank + d) & 15
        return remote(ps.at[peer >> 3, peer & 7], pr.at[rank], ps_sem.at[d], pr_sem.at[rank], member_at(peer))

    def update():
        for way in range(2):
            zsum_copy(1 - way, 1).wait_recv()
            zsum_copy(way, 2).wait_recv()
            g = sums[SLOT[0, 0], core, :, half(way)] + (decode(zr.at[1 - way, 1]) + decode(zr.at[way, 2]))
            first = BETA_FIRST * mt[0, :, half(way)] + (1.0 - BETA_FIRST) * g
            second = BETA_SECOND * mt[1, :, half(way)] + (1.0 - BETA_SECOND) * g * g
            mt[0, :, half(way)] = first
            mt[1, :, half(way)] = second
            powers = []
            encode_blocks(first, 0, powers, ps.at[way])
            encode_blocks(second, 1, powers, ps.at[way])
            encode_powers(powers, ps.at[way])
        lax.fori_loop(1, 16, lambda d, c: (p_copy(d).start(), c)[1], 0)
        pr[rank] = ps[core, t]
        nf[...] = mt[0].T
        ns[...] = mt[1].T

    def project(slot):
        partner_arrived(slot)
        acc[...] += jnp.dot(nb[slot], wb[slot].reshape(512, 256), preferred_element_type=jnp.float32)

    actions = {"z_near": z_near, "z_far": z_far, "moments": transpose_moments, "update": update}
    for k in range(4):
        actions[f"spread_{k}"] = lambda k=k: spread(k)
        actions[f"near_{k}"] = lambda k=k: y_near(k)
        actions[f"far_{k}"] = lambda k=k: y_far(k)
        actions[f"z_{k}"] = lambda k=k: z_sum(k)
        for s in range(4):
            actions[f"y_{k}_{s}"] = lambda k=k, s=s: y_sum(k, s)

    def events(j, low, high):
        for step, names in STEPS.items():
            if low <= step < high:

                @pl.when(j == step)
                def _():
                    for name in names.split():
                        actions[name]()

    own_cot.start()
    rows = [((z + d) & 3) << 11 for d in range(4)]
    places = [((y + d) & 3) << 9 for d in range(4)]
    loads = [load_pair(SLOT[oz, oy], pl.multiple_of(rows[oz] + places[oy], 512)) for oz, oy in SEQUENCE]
    loads[0].start()
    own_w.start()
    for load in loads[1:]:
        load.start()
    own_m1.start()
    own_m2.start()
    own_points.start()

    barrier = pltpu.get_barrier_semaphore()
    for device in (*y_to, *z_to):
        pl.semaphore_signal(barrier, inc=1, device_id=device, device_id_type=MESH)
    for d in range(1, 16):
        pl.semaphore_signal(barrier, inc=1, device_id=member_at((rank + d) & 15), device_id_type=MESH)
    own_cot.wait()
    ct[...] = cb[...].astype(jnp.float32).T.astype(jnp.bfloat16)

    def first_loop(j, carry):
        gradient(j)

        @pl.when(j >= 3)
        def _():
            add_partner(j - 3)

        events(j, 0, 16)
        return carry

    lax.fori_loop(0, 16, first_loop, 0)
    acc[...] = jnp.zeros_like(acc)
    par[...] = jnp.zeros_like(par)

    def second_loop(j, carry):
        @pl.when(j < 19)
        def _():
            add_partner(j - 3)

        events(j, 16, LAST)

        @pl.when((j >= PROJECT) & (j < PROJECT + 16))
        def _():
            project(15 + PROJECT - j)

        return carry

    lax.fori_loop(16, LAST, second_loop, 0)
    kv[...] = acc[...].astype(jnp.bfloat16)

    def member(d, carry):
        r = (rank + 16 - d) & 15

        @pl.when(d > 0)
        def _():
            remote(ps.at[core, t], pr.at[r], ps_sem.at[d], pr_sem.at[r], partner).wait_recv()

        blocks = decode_block(pr.at[r])
        for i in range(PARITY):
            gap = jnp.full((32, 128), points[i] - points[PARITY + r], jnp.int32).astype(jnp.float32)
            weight = 1.0 / gap
            for kind in range(2):
                par[i, kind] += weight * blocks[kind]
        return carry

    lax.fori_loop(0, 16, member, 0)

    def sent_slot(slot, carry):
        x_copy(slot).wait_send()
        partner_copy(slot).wait_send()
        return carry

    lax.fori_loop(0, 16, sent_slot, 0)
    for way in range(2):
        for g in range(4):
            y_copy(g, 0, way).wait_send()
            y_copy(g, 3 if way == 0 else 1, way).wait_send()
            for s in range(3):
                ysum_copy(way, g, s).wait_send()
        z_copy(0, way).wait_send()
        z_copy(3 if way == 0 else 1, way).wait_send()
        for s in range(3):
            zsum_copy(way, s).wait_send()
    lax.fori_loop(1, 16, lambda d, c: (p_copy(d).wait_send(), c)[1], 0)


STEPS = {
    3: "y_0_0",
    6: "y_0_1",
    8: "y_2_0",
    10: "y_1_0",
    11: "y_0_2 near_0",
    13: "y_2_1 y_1_1",
    15: "moments",
    16: "y_0_3",
    17: "y_3_0",
    18: "z_near",
    19: "y_2_2",
    21: "z_0",
    22: "far_0 y_1_2",
    24: "spread_3",
    27: "y_3_2",
    28: "spread_1 y_2_3",
    29: "y_3_1 z_1",
    30: "z_far y_1_3",
    31: "z_2",
    32: "spread_2 near_3 near_1",
    33: "y_3_3",
    34: "near_2 update",
    35: "far_3",
    36: "far_1",
    37: "far_2",
}
PROJECT = 26
LAST = 42


def hand_out(*refs):
    half = len(refs) // 2
    for source, target in zip(refs[:half], refs[half:]):
        target[...] = source[...]


def local(normed, kv_weight, kv_cotangent, first_moment, second_moment, cauchy_points):
    hbm = pl.BlockSpec(memory_space=pltpu.HBM)
    vmem = pl.BlockSpec(memory_space=pltpu.VMEM)
    dma = pltpu.SemaphoreType.DMA
    shapes = (
        jax.ShapeDtypeStruct((1024, 256), jnp.bfloat16),
        jax.ShapeDtypeStruct((256, 256), jnp.float32),
        jax.ShapeDtypeStruct((256, 256), jnp.float32),
        jax.ShapeDtypeStruct((PARITY, 2, 32, 128), jnp.float32),
    )
    results = pl.pallas_call(
        kernel,
        out_shape=shapes,
        in_specs=[hbm] * 6,
        out_specs=(vmem,) * 4,
        scratch_shapes=[
            pltpu.VMEM((16, 1024, 512), jnp.bfloat16),
            pltpu.VMEM((16, 2, 256, 256), jnp.bfloat16),
            pltpu.VMEM((1024, 256), jnp.bfloat16),
            pltpu.VMEM((256, 1024), jnp.bfloat16),
            pltpu.VMEM((2, 256, 256), jnp.float32),
            pltpu.VMEM((2, 256, 256), jnp.float32),
            pltpu.VMEM((16, 2, 256, 256), jnp.float32),
            pltpu.VMEM((16, 272, 256), jnp.int16),
            pltpu.VMEM((16, 272, 256), jnp.int16),
            pltpu.VMEM((2, 4, 3, 272, 128), jnp.int16),
            pltpu.VMEM((2, 4, 3, 272, 128), jnp.int16),
            pltpu.VMEM((2, 3, 272, 128), jnp.int16),
            pltpu.VMEM((2, 3, 272, 128), jnp.int16),
            pltpu.VMEM((1024, 256), jnp.float32),
            pltpu.VMEM((2, 8, 80, 128), jnp.int16),
            pltpu.VMEM((16, 80, 128), jnp.int16),
            pltpu.SMEM((20,), jnp.int32),
            dma((16,)),
            dma((5,)),
            dma((16,)),
            dma((16,)),
            dma((2, 4, 3)),
            dma((2, 4, 3)),
            dma((2, 3)),
            dma((2, 3)),
            dma((16, 2)),
            dma((16, 2)),
            dma((16, 2)),
            dma((16,)),
            dma((16,)),
            dma((16,)),
            dma((16,)),
        ],
        compiler_params=pltpu.CompilerParams(
            collective_id=0, has_side_effects=True, vmem_limit_bytes=46 * 1024 * 1024
        ),
    )(*[pltpu.with_memory_space_constraint(v, pltpu.HBM) for v in (normed, kv_weight, kv_cotangent, first_moment, second_moment, cauchy_points)])
    kv, nf, ns, par = pl.pallas_call(
        hand_out,
        out_shape=shapes,
        in_specs=[vmem] * 4,
        out_specs=(vmem,) * 4,
        compiler_params=pltpu.CompilerParams(vmem_limit_bytes=8 * 1024 * 1024),
    )(*results)
    return kv, nf, ns, par.transpose(0, 1, 3, 2)


def solution(mesh):
    return jax.shard_map(
        local,
        mesh=mesh,
        in_specs=(
            P("fsdp", None),
            P("fsdp", "tp"),
            P("fsdp", "tp"),
            P("fsdp", "tp"),
            P("fsdp", "tp"),
            P(),
        ),
        out_specs=(P("fsdp", "tp"), P("fsdp", "tp"), P("fsdp", "tp"), P(None, None, "fsdp", "tp")),
        check_vma=False,
    )
```
